32 devices in a mesh: utt: 4 (over y, core), clu: 8 (over z, x).
Axes of the slice: x: 2, y: 2, z: 4, core: 2. Of those that a mesh axis runs over, the one named last changes fastest.
Arguments:
- features: bfloat16 [65536, 1280], P(('utt', 'clu')), may hold values from -1.75 to 1.75
- centroids: bfloat16 [1024, 1280], P('clu'), may hold values from -2 to 2
- route: int32 [32, 32], P(('utt', 'clu')), may hold values from 0 to 31, each once within a row
Outputs:
- trainer_labels: int32 [32, 32, 64], P(('utt', 'clu'))
- trainer_distance: float32 [32, 32, 64], P(('utt', 'clu'))
The draws below stay inside these ranges and needn't reach their ends.
Inputs may be any that keep to these rules, and one draw needn't show every extreme that they name: Each row of route names every trainer device exactly once.
All inputs are finite; a program needn't handle non-finite values.
Results may differ from the reference program's by a relative error of at most 0.0003.
Values may be sent and summed in bfloat16 or wider, within the bound.
A program may use at most 64 MiB of HBM per device.

```python
import jax
import jax.numpy as jnp
from jax import lax

D = 1280
K = 1024
FRAMES = 65536
DEVICES = 32


def joint_draw(key):
    base = jax.random.fold_in(key, 7)
    k_cent, k_pick, k_mask, k_noise = jax.random.split(base, 4)
    cent_int = jax.random.randint(k_cent, (K, D), -128, 129)
    noise = jax.random.randint(k_noise, (FRAMES, D), -10, 11)
    keep = jax.random.randint(k_mask, (FRAMES, D), 0, 4) == 0
    picks = jax.random.randint(k_pick, (FRAMES,), 0, K)
    signal = jnp.where(keep, cent_int[picks] // 32, 0)
    feat_int = signal + noise
    feats = feat_int.astype(jnp.float32) / 8.0
    cent = cent_int.astype(jnp.float32) / 64.0
    return (feats, cent)


def draw_features(key, part):
    return joint_draw(key)[0].astype(jnp.bfloat16)


def draw_centroids(key, part):
    return joint_draw(key)[1].astype(jnp.bfloat16)


def setup_inputs(seed: int = 0) -> dict:
    arg_keys = jax.random.split(jax.random.key(seed), 4)
    features = draw_features(jax.random.fold_in(arg_keys[3], 71), 0)
    centroids = draw_centroids(jax.random.fold_in(arg_keys[3], 71), 0)
    route = jax.vmap(lambda own: jax.random.permutation(own, DEVICES))(jax.random.split(arg_keys[2], DEVICES)).reshape((DEVICES, DEVICES)).astype(jnp.int32)
    return {"features": features, "centroids": centroids, "route": route}


def reference(features, centroids, route):
    cent_sq = jnp.sum(jnp.square(centroids.astype(jnp.float32)), axis=1)
    step = 1024
    blocks = features.reshape(FRAMES // step, step, D)

    def nearest(block):
        frame_sq = jnp.sum(jnp.square(block.astype(jnp.float32)), axis=1)
        inner = jnp.dot(block, centroids.T, preferred_element_type=jnp.float32)
        dist = (frame_sq[:, None] - 2.0 * inner + cent_sq[None, :]) / D
        return jnp.argmin(dist, axis=1).astype(jnp.int32), jnp.min(dist, axis=1)

    labels, least = lax.map(nearest, blocks)
    devices = route.shape[0]
    labels = labels.reshape(devices, devices, FRAMES // (devices * devices))
    least = least.reshape(devices, devices, FRAMES // (devices * devices))
    inverse = jnp.argsort(route, axis=1).astype(jnp.int32)
    picked_labels = jnp.take_along_axis(labels, inverse[:, :, None], axis=1)
    picked_least = jnp.take_along_axis(least, inverse[:, :, None], axis=1)
    return jnp.transpose(picked_labels, (1, 0, 2)), jnp.transpose(picked_least, (1, 0, 2))
```

```python
import functools

import jax
import jax.numpy as jnp
from jax import lax
from jax.experimental import pallas as pl
from jax.experimental.pallas import tpu as pltpu
from jax.sharding import PartitionSpec as P

LANES = 128


def lane_sums(rows):
    wide = rows.astype(jnp.float32)
    wide = wide * wide
    part = wide[:, :LANES]
    for j in range(1, rows.shape[1] // LANES):
        part = part + wide[:, j * LANES:(j + 1) * LANES]
    return jnp.sum(part.T, axis=0, keepdims=True)


def kernel(n_utt, n_clu, n_x, feat_hbm, cent_hbm, route_ref, lab_out, dist_out,
           feat, cent, val, idx, fsq, csq, res, sent, got,
           feat_sem, own_sem, z_send, z_recv, x_send, x_recv, c_send, c_recv, a_send, a_recv):
    n_z = n_clu // n_x
    devices = n_utt * n_clu
    utt, clu = lax.axis_index("utt"), lax.axis_index("clu")
    me = utt * n_clu + clu
    half, x, z = utt % 2, clu % n_x, clu // n_x
    frames, width = feat.shape
    tile = frames // feat_sem.shape[0]
    per_block = frames // devices

    def xor(a, b):
        out, bit = a, 1
        while bit <= b:
            if b & bit:
                out = out + bit * (1 - 2 * ((a // bit) % 2))
            bit *= 2
        return out

    def slot(r, s):
        return xor(z, r) * n_x + xor(x, s)

    partner = xor(utt, 1)
    own = pltpu.make_async_copy(cent_hbm, cent.at[clu], own_sem)
    own.start()

    def feat_copy(t):
        span = pl.ds(t * tile, tile)
        return pltpu.make_async_copy(feat_hbm.at[span], feat.at[span], feat_sem.at[t])

    for t in range(frames // tile):
        feat_copy(t).start()

    barrier = pltpu.get_barrier_semaphore()

    def greet(j, carry):
        other = lax.rem(me + j, devices)
        pl.semaphore_signal(barrier, inc=1, device_id=(other // n_clu, other % n_clu),
                            device_id_type=pl.DeviceIdType.MESH)
        return carry

    lax.fori_loop(1, devices, greet, 0)

    def remote(piece, send, recv, u, w):
        return pltpu.make_async_remote_copy(src_ref=piece, dst_ref=piece, send_sem=send, recv_sem=recv,
                                            device_id=(u, w), device_id_type=pl.DeviceIdType.MESH)

    def z_copy(r, incoming=False):
        piece = cent.at[slot(r, 0) if incoming else clu, half]
        return remote(piece, z_send.at[r], z_recv.at[r], utt, slot(r, 0))

    def x_copy(r, s, incoming=False):
        piece = cent.at[slot(r, s if incoming else 0), half]
        return remote(piece, x_send.at[r, s], x_recv.at[r, s], utt, slot(0, s))

    def c_copy(r, s, incoming=False):
        piece = cent.at[slot(r, s), (1 - half) if incoming else half]
        return remote(piece, c_send.at[r, s], c_recv.at[r, s], partner, clu)

    own.wait()
    pl.semaphore_wait(barrier, devices - 1)
    for s in range(1, n_x):
        x_copy(0, s).start()
    for r in range(1, n_z):
        z_copy(r).start()

    def relay_z(r):
        z_copy(r, True).wait_recv()
        for s in range(1, n_x):
            x_copy(r, s).start()
        c_copy(r, 0).start()

    def relay_x(r):
        for s in range(1, n_x):
            x_copy(r, s, True).wait_recv()
            c_copy(r, s).start()

    def block(w):
        return cent[w].reshape(-1, width)

    def compute(chunks, first=False):
        for i, w in enumerate(chunks):
            csq[0:1, i * LANES:(i + 1) * LANES] = lane_sums(block(w))
        n = len(chunks)
        step = 512

        @pl.loop(0, frames // step)
        def _(t):
            span = pl.ds(pl.multiple_of(t * step, step), step)
            rhs = block(chunks[0]) if n == 1 else jnp.concatenate([block(w) for w in chunks], axis=0)
            inner = lax.dot_general(feat[span, :], rhs, (((1,), (1,)), ((), ())),
                                    preferred_element_type=jnp.float32)
            d = csq[0:1, :n * LANES] - 2.0 * inner
            if first:
                v, k = d[:, :LANES], jnp.full((step, LANES), chunks[0], jnp.int32)
            else:
                v, k = val[span, :], idx[span, :]
            for i in range(1 if first else 0, n):
                new = d[:, i * LANES:(i + 1) * LANES]
                better = (new < v) | ((new == v) & (chunks[i] < k))
                v = jnp.where(better, new, v)
                k = jnp.where(better, chunks[i], k)
            val[span, :] = v
            idx[span, :] = k

    for t in range(frames // tile):
        feat_copy(t).wait()
    compute([slot(0, 0)], first=True)
    relay_x(0)
    relay_z(1)

    @pl.loop(0, frames // LANES)
    def _(t):
        fsq[t] = lane_sums(feat[pl.ds(pl.multiple_of(t * LANES, LANES), LANES), :])

    for r in range(n_z):
        pairs = [(r, s) for s in range(1, n_x)] + ([(r + 1, 0)] if r + 1 < n_z else [])
        for pair in pairs:
            c_copy(*pair, True).wait_recv()
        compute([slot(*pair) for pair in pairs])
        if r + 1 < n_z:
            relay_x(r + 1)
        if r + 2 < n_z:
            relay_z(r + 2)

    lane = lax.broadcasted_iota(jnp.int32, (1, LANES), 1)
    blocks = LANES // per_block

    @pl.loop(0, frames // LANES)
    def _(t):
        span = pl.ds(pl.multiple_of(t * LANES, LANES), LANES)
        v = val[span, :].T
        k = (idx[span, :] * LANES + lax.broadcasted_iota(jnp.int32, (LANES, LANES), 1)).astype(jnp.float32).T
        least = jnp.min(v, axis=0, keepdims=True)
        label = jnp.min(jnp.where(v == least, k, float(n_clu * LANES)), axis=0, keepdims=True)
        dist = (fsq[t] + least) / width
        for j in range(blocks):
            a = label if j == 0 else pltpu.roll(label, LANES - per_block * j, 1)
            shift = (per_block - per_block * j) % LANES
            b = dist if shift == 0 else pltpu.roll(dist, shift, 1)
            res[pl.ds(t * blocks + j, 1), :] = jnp.where(lane < per_block, a, b)

    pick = (route_ref[...] == lax.broadcasted_iota(jnp.int32, (devices, devices), 0)).astype(jnp.float32)
    sent[...] = jnp.dot(pick, res[...], preferred_element_type=jnp.float32,
                        precision=lax.Precision.HIGHEST).reshape(sent.shape)

    def out_copy(j, incoming):
        dst = lax.rem(me + j, devices)
        src = lax.rem(me + devices - j, devices)
        return pltpu.make_async_remote_copy(
            src_ref=sent.at[dst], dst_ref=got.at[src if incoming else me],
            send_sem=a_send.at[j], recv_sem=a_recv.at[j],
            device_id=(dst // n_clu, dst % n_clu), device_id_type=pl.DeviceIdType.MESH)

    def send(j, carry):
        out_copy(j, False).start()
        return carry

    lax.fori_loop(1, devices, send, 0)
    got[me] = sent[me]
    for r in range(n_z):
        for s in range(n_x):
            if s:
                x_copy(r, s).wait_send()
            elif r:
                z_copy(r).wait_send()
            if r or s:
                c_copy(r, s).wait_send()

    def receive(j, carry):
        out_copy(j, True).wait_recv()
        return carry

    lax.fori_loop(1, devices, receive, 0)
    table = got[...].reshape(devices, LANES)
    lab_out[...] = table[:, :per_block].astype(jnp.int32)
    dist_out[...] = table[:, per_block:2 * per_block]

    def sent_off(j, carry):
        out_copy(j, False).wait_send()
        return carry

    lax.fori_loop(1, devices, sent_off, 0)


def per_device(n_utt, n_clu, features, centroids, route):
    frames, width = features.shape
    rows = centroids.shape[0]
    devices = n_utt * n_clu
    n_x = 1
    while n_x * n_x * 4 <= n_clu:
        n_x *= 2
    n_z = n_clu // n_x
    per_block = frames // devices
    tiles = 4
    dma = pltpu.SemaphoreType.DMA
    cent = centroids.reshape(2, rows // 2, width)
    labels, least = pl.pallas_call(
        functools.partial(kernel, n_utt, n_clu, n_x),
        out_shape=(jax.ShapeDtypeStruct((devices, per_block), jnp.int32),
                   jax.ShapeDtypeStruct((devices, per_block), jnp.float32)),
        in_specs=[pl.BlockSpec(memory_space=pl.ANY), pl.BlockSpec(memory_space=pl.ANY),
                  pl.BlockSpec(memory_space=pltpu.VMEM)],
        out_specs=(pl.BlockSpec(memory_space=pltpu.VMEM), pl.BlockSpec(memory_space=pltpu.VMEM)),
        scratch_shapes=[
            pltpu.VMEM((frames, width), features.dtype),
            pltpu.VMEM((n_clu, 2, rows // 2, width), centroids.dtype),
            pltpu.VMEM((frames, LANES), jnp.float32),
            pltpu.VMEM((frames, LANES), jnp.int32),
            pltpu.VMEM((frames // LANES, 1, LANES), jnp.float32),
            pltpu.VMEM((8, n_x * LANES), jnp.float32),
            pltpu.VMEM((devices, LANES), jnp.float32),
            pltpu.VMEM((devices, 1, LANES), jnp.float32),
            pltpu.VMEM((devices, 1, LANES), jnp.float32),
            dma((tiles,)), dma(()),
            dma((n_z,)), dma((n_z,)),
            dma((n_z, n_x)), dma((n_z, n_x)),
            dma((n_z, n_x)), dma((n_z, n_x)),
            dma((devices,)), dma((devices,)),
        ],
        compiler_params=pltpu.CompilerParams(
            collective_id=0, has_side_effects=True, vmem_limit_bytes=60 * 1024 * 1024),
        name="nearest",
    )(features, cent, route)
    return labels.reshape(1, devices, per_block), least.reshape(1, devices, per_block)


def solution(mesh):
    placed = (P(("utt", "clu"), None), P("clu", None), P(("utt", "clu"), None))
    return jax.shard_map(
        functools.partial(per_device, mesh.shape["utt"], mesh.shape["clu"]),
        mesh=mesh,
        in_specs=placed,
        out_specs=(P(("utt", "clu"), None, None), P(("utt", "clu"), None, None)),
        check_vma=False,
    )
```

```python
import functools

import jax
import jax.numpy as jnp
from jax import lax
from jax.experimental import pallas as pl
from jax.experimental.pallas import tpu as pltpu
from jax.sharding import PartitionSpec as P

LANES = 128


def lane_sums(rows):
    wide = rows.astype(jnp.float32)
    wide = wide * wide
    part = wide[:, :LANES]
    for j in range(1, rows.shape[1] // LANES):
        part = part + wide[:, j * LANES:(j + 1) * LANES]
    return jnp.sum(part.T, axis=0, keepdims=True)


def kernel(n_utt, n_clu, n_x, feat_hbm, cent_hbm, route_ref, out,
           feat, cent, val, idx, fsq, csq, res, sent, got,
           feat_sem, own_sem, z_send, z_recv, x_send, x_recv, y_send, y_recv, c_send, c_recv, a_send, a_recv):
    n_z = n_clu // n_x
    devices = n_utt * n_clu
    utt, clu = lax.axis_index("utt"), lax.axis_index("clu")
    me = utt * n_clu + clu
    n_y = n_utt // 2
    half, y, x, z = utt % 2, utt // 2, clu % n_x, clu // n_x
    frames, width = feat.shape
    tile = frames // feat_sem.shape[0]
    per_block = frames // devices

    def xor(a, b):
        out, bit = a, 1
        while bit <= b:
            if b & bit:
                out = out + bit * (1 - 2 * ((a // bit) % 2))
            bit *= 2
        return out

    def slot(r, s):
        return xor(z, r) * n_x + xor(x, s)

    partner = xor(utt, 1)
    own = pltpu.make_async_copy(cent_hbm, cent.at[clu], own_sem)
    own.start()

    def feat_copy(t):
        span = pl.ds(t * tile, tile)
        return pltpu.make_async_copy(feat_hbm.at[span], feat.at[span], feat_sem.at[t])

    for t in range(frames // tile):
        feat_copy(t).start()

    barrier = pltpu.get_barrier_semaphore()
    peers = ([(utt, slot(r, 0)) for r in range(1, n_z)] + [(utt, slot(0, s)) for s in range(1, n_x)]
             + [(xor(utt, 2 * t), clu) for t in range(1, n_y)] + [(partner, clu)])
    for peer in peers:
        pl.semaphore_signal(barrier, inc=1, device_id=peer, device_id_type=pl.DeviceIdType.MESH)

    def remote(piece, send, recv, u, w):
        return pltpu.make_async_remote_copy(src_ref=piece, dst_ref=piece, send_sem=send, recv_sem=recv,
                                            device_id=(u, w), device_id_type=pl.DeviceIdType.MESH)

    def z_copy(r, incoming=False):
        piece = cent.at[slot(r, 0) if incoming else clu, half, y]
        return remote(piece, z_send.at[r], z_recv.at[r], utt, slot(r, 0))

    def x_copy(r, s, incoming=False):
        piece = cent.at[slot(r, s if incoming else 0), half]
        return remote(piece.at[y] if r else piece, x_send.at[r, s], x_recv.at[r, s], utt, slot(0, s))

    def y_copy(r, s, t, incoming=False):
        piece = cent.at[slot(r, s), half, xor(y, t) if incoming else y]
        return remote(piece, y_send.at[r, s, t], y_recv.at[r, s, t], xor(utt, 2 * t), clu)

    def c_copy(r, s, incoming=False):
        piece = cent.at[slot(r, s), (1 - half) if incoming else half]
        return remote(piece, c_send.at[r, s], c_recv.at[r, s], partner, clu)

    own.wait()
    pl.semaphore_wait(barrier, len(peers))
    for s in range(1, n_x):
        x_copy(0, s).start()
    for r in range(1, n_z):
        z_copy(r).start()

    def relay_z(r):
        if r < n_z:
            z_copy(r, True).wait_recv()
            for s in range(1, n_x):
                x_copy(r, s).start()
            for t in range(1, n_y):
                y_copy(r, 0, t).start()

    def relay_x(r):
        if r < n_z:
            for s in range(1, n_x):
                x_copy(r, s, True).wait_recv()
                if r:
                    for t in range(1, n_y):
                        y_copy(r, s, t).start()
                else:
                    c_copy(r, s).start()

    def relay_y(r, s):
        if 0 < r < n_z:
            for t in range(1, n_y):
                y_copy(r, s, t, True).wait_recv()
            c_copy(r, s).start()

    def block(w):
        return cent[w].reshape(-1, width)

    lane = lax.broadcasted_iota(jnp.int32, (1, LANES), 1)
    blocks = LANES // per_block
    step = 512

    def finish(t, v, k):
        v = v.T
        k = (k * LANES + lane).astype(jnp.float32).T
        least = jnp.min(v, axis=0, keepdims=True)
        label = jnp.min(jnp.where(v == least, k, float(n_clu * LANES)), axis=0, keepdims=True)
        dist = (fsq[t] + least) / width
        for j in range(blocks):
            a = label if j == 0 else pltpu.roll(label, LANES - per_block * j, 1)
            shift = (per_block - per_block * j) % LANES
            b = dist if shift == 0 else pltpu.roll(dist, shift, 1)
            res[pl.ds(t * blocks + j, 1), :] = jnp.where(lane < per_block, a, b)

    def compute(chunks, start, stop, first=False, last=False):
        n = len(chunks)
        if start == 0:
            for i, w in enumerate(chunks):
                csq[0:1, i * LANES:(i + 1) * LANES] = lane_sums(block(w))

        @pl.loop(start, stop)
        def _(t):
            span = pl.ds(pl.multiple_of(t * step, step), step)
            rhs = block(chunks[0]) if n == 1 else jnp.concatenate([block(w) for w in chunks], axis=0)
            inner = lax.dot_general(feat[span, :], rhs, (((1,), (1,)), ((), ())),
                                    preferred_element_type=jnp.float32)
            d = csq[0:1, :n * LANES] - 2.0 * inner
            if first:
                v, k = d[:, :LANES], jnp.full((step, LANES), chunks[0], jnp.int32)
            else:
                v, k = val[span, :], idx[span, :]
            for i in range(1 if first else 0, n):
                new = d[:, i * LANES:(i + 1) * LANES]
                better = (new < v) | ((new == v) & (chunks[i] < k))
                v = jnp.where(better, new, v)
                k = jnp.where(better, chunks[i], k)
            if last:
                for i in range(step // LANES):
                    part = slice(i * LANES, (i + 1) * LANES)
                    finish(t * (step // LANES) + i, v[part], k[part])
            else:
                val[span, :] = v
                idx[span, :] = k

    def squares(start, stop):
        @pl.loop(start, stop)
        def _(t):
            fsq[t] = lane_sums(feat[pl.ds(pl.multiple_of(t * LANES, LANES), LANES), :])

    for t in range(frames // tile):
        feat_copy(t).wait()
    steps, tiles = frames // step, frames // LANES
    compute([slot(0, 0)], 0, steps, first=True)
    relay_z(1)
    squares(0, tiles // 2)
    relay_x(0)
    relay_y(1, 0)
    squares(tiles // 2, tiles)
    relay_z(2)
    relay_x(1)
    for r in range(n_z):
        pairs = [(r, s) for s in range(1, n_x)] + ([(r + 1, 0)] if r + 1 < n_z else [])
        for pair in pairs:
            c_copy(*pair, True).wait_recv()
        chunks = [slot(*pair) for pair in pairs]
        last = r + 1 == n_z
        compute(chunks, 0, steps // 2, last=last)
        relay_z(r + 3)
        relay_x(r + 2)
        compute(chunks, steps // 2, steps, last=last)
        relay_y(r + 2, 0)
        for s in range(1, n_x):
            relay_y(r + 1, s)

    pick = (route_ref[...] == lax.broadcasted_iota(jnp.int32, (devices, devices), 0)).astype(jnp.float32)
    sent[...] = jnp.dot(pick, res[...], preferred_element_type=jnp.float32,
                        precision=lax.Precision.HIGHEST).reshape(sent.shape)

    def out_copy(j, incoming):
        dst = lax.rem(me + j, devices)
        src = lax.rem(me + devices - j, devices)
        return pltpu.make_async_remote_copy(
            src_ref=sent.at[dst], dst_ref=got.at[src if incoming else me],
            send_sem=a_send.at[j], recv_sem=a_recv.at[j],
            device_id=(dst // n_clu, dst % n_clu), device_id_type=pl.DeviceIdType.MESH)

    def send(j, carry):
        out_copy(j, False).start()
        return carry

    lax.fori_loop(1, devices, send, 0)
    got[me] = sent[me]
    for r in range(n_z):
        for s in range(n_x):
            if s:
                x_copy(r, s).wait_send()
            elif r:
                z_copy(r).wait_send()
            if r:
                for t in range(1, n_y):
                    y_copy(r, s, t).wait_send()
            if r or s:
                c_copy(r, s).wait_send()

    def receive(j, carry):
        out_copy(j, True).wait_recv()
        return carry

    lax.fori_loop(1, devices, receive, 0)
    out[...] = got[...].reshape(devices, LANES)

    def sent_off(j, carry):
        out_copy(j, False).wait_send()
        return carry

    lax.fori_loop(1, devices, sent_off, 0)


def per_device(n_utt, n_clu, features, centroids, route):
    frames, width = features.shape
    rows = centroids.shape[0]
    devices = n_utt * n_clu
    n_x = 1
    while n_x * n_x * 4 <= n_clu:
        n_x *= 2
    n_z = n_clu // n_x
    per_block = frames // devices
    tiles = 4
    dma = pltpu.SemaphoreType.DMA
    n_y = n_utt // 2
    cent = centroids.reshape(2, n_y, rows // n_utt, width)
    table = pl.pallas_call(
        functools.partial(kernel, n_utt, n_clu, n_x),
        out_shape=jax.ShapeDtypeStruct((devices, LANES), jnp.float32),
        in_specs=[pl.BlockSpec(memory_space=pl.ANY), pl.BlockSpec(memory_space=pl.ANY),
                  pl.BlockSpec(memory_space=pltpu.VMEM)],
        out_specs=pl.BlockSpec(memory_space=pltpu.VMEM),
        scratch_shapes=[
            pltpu.VMEM((frames, width), features.dtype),
            pltpu.VMEM((n_clu,) + cent.shape, centroids.dtype),
            pltpu.VMEM((frames, LANES), jnp.float32),
            pltpu.VMEM((frames, LANES), jnp.int32),
            pltpu.VMEM((frames // LANES, 1, LANES), jnp.float32),
            pltpu.VMEM((8, n_x * LANES), jnp.float32),
            pltpu.VMEM((devices, LANES), jnp.float32),
            pltpu.VMEM((devices, 1, LANES), jnp.float32),
            pltpu.VMEM((devices, 1, LANES), jnp.float32),
            dma((tiles,)), dma(()),
            dma((n_z,)), dma((n_z,)),
            dma((n_z, n_x)), dma((n_z, n_x)),
            dma((n_z, n_x, n_y)), dma((n_z, n_x, n_y)),
            dma((n_z, n_x)), dma((n_z, n_x)),
            dma((devices,)), dma((devices,)),
        ],
        compiler_params=pltpu.CompilerParams(
            collective_id=0, has_side_effects=True, vmem_limit_bytes=60 * 1024 * 1024),
        name="nearest",
    )(features, cent, route)
    labels, least = table[:, :per_block].astype(jnp.int32), table[:, per_block:2 * per_block]
    return labels.reshape(1, devices, per_block), least.reshape(1, devices, per_block)


def solution(mesh):
    placed = (P(("utt", "clu"), None), P("clu", None), P(("utt", "clu"), None))
    return jax.shard_map(
        functools.partial(per_device, mesh.shape["utt"], mesh.shape["clu"]),
        mesh=mesh,
        in_specs=placed,
        out_specs=(P(("utt", "clu"), None, None), P(("utt", "clu"), None, None)),
        check_vma=False,
    )
```

```python
import functools

import jax
import jax.numpy as jnp
from jax import lax
from jax.experimental import pallas as pl
from jax.experimental.pallas import tpu as pltpu
from jax.sharding import PartitionSpec as P

LANES = 128


def lane_sums(rows):
    wide = rows.astype(jnp.float32)
    wide = wide * wide
    part = wide[:, :LANES]
    for j in range(1, rows.shape[1] // LANES):
        part = part + wide[:, j * LANES:(j + 1) * LANES]
    return jnp.sum(part.T, axis=0, keepdims=True)


def kernel(n_utt, n_clu, n_x, feat_hbm, cent_hbm, route_ref, out,
           feat, cent, val, idx, fsq, csq, res, sent, got,
           feat_sem, own_sem, d_send, d_recv, y_send, y_recv, c_send, c_recv, a_send, a_recv):
    n_z = n_clu // n_x
    devices = n_utt * n_clu
    utt, clu = lax.axis_index("utt"), lax.axis_index("clu")
    me = utt * n_clu + clu
    n_y = n_utt // 2
    half, y, x, z = utt % 2, utt // 2, clu % n_x, clu // n_x
    frames, width = feat.shape
    tile = frames // feat_sem.shape[0]
    per_block = frames // devices

    def xor(a, b):
        out, bit = a, 1
        while bit <= b:
            if b & bit:
                out = out + bit * (1 - 2 * ((a // bit) % 2))
            bit *= 2
        return out

    def slot(r, s):
        return xor(z, r) * n_x + xor(x, s)

    partner = xor(utt, 1)
    own = pltpu.make_async_copy(cent_hbm, cent.at[clu], own_sem)
    own.start()

    def feat_copy(t):
        span = pl.ds(t * tile, tile)
        return pltpu.make_async_copy(feat_hbm.at[span], feat.at[span], feat_sem.at[t])

    for t in range(frames // tile):
        feat_copy(t).start()

    barrier = pltpu.get_barrier_semaphore()
    peers = ([(utt, slot(r, s)) for r in range(n_z) for s in range(n_x) if r or s]
             + [(xor(utt, 2 * t), clu) for t in range(1, n_y)] + [(partner, clu)])
    for peer in peers:
        pl.semaphore_signal(barrier, inc=1, device_id=peer, device_id_type=pl.DeviceIdType.MESH)

    def remote(piece, send, recv, u, w):
        return pltpu.make_async_remote_copy(src_ref=piece, dst_ref=piece, send_sem=send, recv_sem=recv,
                                            device_id=(u, w), device_id_type=pl.DeviceIdType.MESH)

    odd, even = range(1, n_z, 2), range(2, n_z, 2)
    cols = range(1, n_x)
    split = [(r, s) for r in odd for s in cols] + [(r, s) for r in even for s in range(n_x)]

    def d_copy(r, s, incoming=False):
        relayed = s > 0 and r > 0 and r % 2 == 0
        if incoming:
            piece = cent.at[slot(r, s), half]
        else:
            piece = cent.at[slot(r, 0) if relayed else clu, half]
        if (r, s) in split:
            piece = piece.at[y]
        return remote(piece, d_send.at[r, s], d_recv.at[r, s], utt, slot(0 if relayed else r, s))

    def y_copy(r, s, t, incoming=False):
        piece = cent.at[slot(r, s), half, xor(y, t) if incoming else y]
        return remote(piece, y_send.at[r, s, t], y_recv.at[r, s, t], xor(utt, 2 * t), clu)

    def c_copy(r, s, incoming=False):
        piece = cent.at[slot(r, s), (1 - half) if incoming else half]
        return remote(piece, c_send.at[r, s], c_recv.at[r, s], partner, clu)

    own.wait()
    pl.semaphore_wait(barrier, len(peers))
    for s in cols:
        d_copy(0, s).start()
    for r in even:
        d_copy(r, 0).start()
    for r in odd:
        d_copy(r, 0).start()
    for r in odd:
        for s in cols:
            d_copy(r, s).start()

    def landed(pieces):
        for r, s in pieces:
            d_copy(r, s, True).wait_recv()
            if (r, s) in split:
                if s == 0:
                    for j in cols:
                        d_copy(r, j).start()
                for t in range(1, n_y):
                    y_copy(r, s, t).start()
            else:
                c_copy(r, s).start()

    def joined(pieces):
        for r, s in pieces:
            for t in range(1, n_y):
                y_copy(r, s, t, True).wait_recv()
            c_copy(r, s).start()

    def ready(pieces):
        for r, s in pieces:
            c_copy(r, s, True).wait_recv()
        return [slot(r, s) for r, s in pieces]

    def block(w):
        return cent[w].reshape(-1, width)

    lane = lax.broadcasted_iota(jnp.int32, (1, LANES), 1)
    blocks = LANES // per_block
    step = 512

    def finish(t, v, k):
        v = v.T
        k = (k * LANES + lane).astype(jnp.float32).T
        least = jnp.min(v, axis=0, keepdims=True)
        label = jnp.min(jnp.where(v == least, k, float(n_clu * LANES)), axis=0, keepdims=True)
        dist = (fsq[t] + least) / width
        for j in range(blocks):
            a = label if j == 0 else pltpu.roll(label, LANES - per_block * j, 1)
            shift = (per_block - per_block * j) % LANES
            b = dist if shift == 0 else pltpu.roll(dist, shift, 1)
            res[pl.ds(t * blocks + j, 1), :] = jnp.where(lane < per_block, a, b)

    def compute(chunks, start, stop, first=False, last=False):
        n = len(chunks)
        if start == 0:
            for i, w in enumerate(chunks):
                csq[0:1, i * LANES:(i + 1) * LANES] = lane_sums(block(w))

        @pl.loop(start, stop)
        def _(t):
            span = pl.ds(pl.multiple_of(t * step, step), step)
            rhs = block(chunks[0]) if n == 1 else jnp.concatenate([block(w) for w in chunks], axis=0)
            inner = lax.dot_general(feat[span, :], rhs, (((1,), (1,)), ((), ())),
                                    preferred_element_type=jnp.float32)
            d = csq[0:1, :n * LANES] - 2.0 * inner
            if first:
                v, k = d[:, :LANES], jnp.full((step, LANES), chunks[0], jnp.int32)
            else:
                v, k = val[span, :], idx[span, :]
            for i in range(1 if first else 0, n):
                new = d[:, i * LANES:(i + 1) * LANES]
                better = (new < v) | ((new == v) & (chunks[i] < k))
                v = jnp.where(better, new, v)
                k = jnp.where(better, chunks[i], k)
            if last:
                for i in range(step // LANES):
                    part = slice(i * LANES, (i + 1) * LANES)
                    finish(t * (step // LANES) + i, v[part], k[part])
            else:
                val[span, :] = v
                idx[span, :] = k

    def squares(start, stop):
        @pl.loop(start, stop)
        def _(t):
            fsq[t] = lane_sums(feat[pl.ds(pl.multiple_of(t * LANES, LANES), LANES), :])

    for t in range(frames // tile):
        feat_copy(t).wait()
    steps, tiles = frames // step, frames // LANES
    compute([slot(0, 0)], 0, steps, first=True)
    squares(0, tiles // 2)
    near = [(0, s) for s in cols]
    sides = [(r, 0) for r in odd]
    far = [(r, 0) for r in even]
    first_col = [(1, s) for s in cols]
    rest_col = [(r, s) for r in odd[1:] for s in cols]
    far_col = [(r, s) for r in even for s in cols]
    landed(near)
    landed(far)
    squares(tiles // 2, tiles)
    chunks = ready(near)
    compute(chunks, 0, steps // 2)
    landed(first_col)
    landed(sides)
    compute(chunks, steps // 2, steps)
    joined(far)
    landed(rest_col)
    landed(far_col)
    chunks = ready(sides)
    compute(chunks, 0, steps // 2)
    joined(first_col)
    compute(chunks, steps // 2, steps)
    joined(rest_col)
    chunks = ready(far + first_col)
    compute(chunks, 0, steps // 2)
    joined(far_col)
    compute(chunks, steps // 2, steps)
    compute(ready(rest_col + far_col), 0, steps, last=True)

    pick = (route_ref[...] == lax.broadcasted_iota(jnp.int32, (devices, devices), 0)).astype(jnp.float32)
    sent[...] = jnp.dot(pick, res[...], preferred_element_type=jnp.float32,
                        precision=lax.Precision.HIGHEST).reshape(sent.shape)

    def out_copy(j, incoming):
        dst = lax.rem(me + j, devices)
        src = lax.rem(me + devices - j, devices)
        return pltpu.make_async_remote_copy(
            src_ref=sent.at[dst], dst_ref=got.at[src if incoming else me],
            send_sem=a_send.at[j], recv_sem=a_recv.at[j],
            device_id=(dst // n_clu, dst % n_clu), device_id_type=pl.DeviceIdType.MESH)

    def send(j, carry):
        out_copy(j, False).start()
        return carry

    lax.fori_loop(1, devices, send, 0, unroll=True)
    got[me] = sent[me]
    for r in range(n_z):
        for s in range(n_x):
            if r or s:
                d_copy(r, s).wait_send()
                c_copy(r, s).wait_send()
            if (r, s) in split:
                for t in range(1, n_y):
                    y_copy(r, s, t).wait_send()

    def receive(j, carry):
        out_copy(j, True).wait_recv()
        return carry

    lax.fori_loop(1, devices, receive, 0)
    out[...] = got[...].reshape(devices, LANES)

    def sent_off(j, carry):
        out_copy(j, False).wait_send()
        return carry

    lax.fori_loop(1, devices, sent_off, 0)


def per_device(n_utt, n_clu, features, centroids, route):
    frames, width = features.shape
    rows = centroids.shape[0]
    devices = n_utt * n_clu
    n_x = 1
    while n_x * n_x * 4 <= n_clu:
        n_x *= 2
    n_z = n_clu // n_x
    per_block = frames // devices
    tiles = 4
    dma = pltpu.SemaphoreType.DMA
    n_y = n_utt // 2
    cent = centroids.reshape(2, n_y, rows // n_utt, width)
    table = pl.pallas_call(
        functools.partial(kernel, n_utt, n_clu, n_x),
        out_shape=jax.ShapeDtypeStruct((devices, LANES), jnp.float32),
        in_specs=[pl.BlockSpec(memory_space=pl.ANY), pl.BlockSpec(memory_space=pl.ANY),
                  pl.BlockSpec(memory_space=pltpu.VMEM)],
        out_specs=pl.BlockSpec(memory_space=pltpu.VMEM),
        scratch_shapes=[
            pltpu.VMEM((frames, width), features.dtype),
            pltpu.VMEM((n_clu,) + cent.shape, centroids.dtype),
            pltpu.VMEM((frames, LANES), jnp.float32),
            pltpu.VMEM((frames, LANES), jnp.int32),
            pltpu.VMEM((frames // LANES, 1, LANES), jnp.float32),
            pltpu.VMEM((8, n_clu * LANES), jnp.float32),
            pltpu.VMEM((devices, LANES), jnp.float32),
            pltpu.VMEM((devices, 1, LANES), jnp.float32),
            pltpu.VMEM((devices, 1, LANES), jnp.float32),
            dma((tiles,)), dma(()),
            dma((n_z, n_x)), dma((n_z, n_x)),
            dma((n_z, n_x, n_y)), dma((n_z, n_x, n_y)),
            dma((n_z, n_x)), dma((n_z, n_x)),
            dma((devices,)), dma((devices,)),
        ],
        compiler_params=pltpu.CompilerParams(
            collective_id=0, has_side_effects=True, vmem_limit_bytes=60 * 1024 * 1024),
        name="nearest",
    )(features, cent, route)
    labels, least = table[:, :per_block].astype(jnp.int32), table[:, per_block:2 * per_block]
    return labels.reshape(1, devices, per_block), least.reshape(1, devices, per_block)


def solution(mesh):
    placed = (P(("utt", "clu"), None), P("clu", None), P(("utt", "clu"), None))
    return jax.shard_map(
        functools.partial(per_device, mesh.shape["utt"], mesh.shape["clu"]),
        mesh=mesh,
        in_specs=placed,
        out_specs=(P(("utt", "clu"), None, None), P(("utt", "clu"), None, None)),
        check_vma=False,
    )
```
